32 devices in a mesh: dp: 8 (over y, x, core), mp: 4 (over z).
Axes of the slice: x: 2, y: 2, z: 4, core: 2. Of those that a mesh axis runs over, the one named last changes fastest.
Arguments:
- pooled: bfloat16 [2048, 3584], P('dp', 'mp'), may hold values from -4 to 4
- w_out: bfloat16 [3584, 3584], P('mp'), may hold values from -0.028931878 to 0.028931878
- assignments: int32 [2048], P('dp'), may hold values from 0 to 4095
- ema_sums: float32 [4096, 3584], P('mp', 'dp'), may hold values from -0.40089186 to 0.40089186
- ema_counts: float32 [4096], P('mp'), may hold values from 1 to 8
Outputs:
- distances: float32 [2048, 4096], P('dp', 'mp')
- new_sums: float32 [4096, 3584], P('mp', 'dp')
- new_counts: float32 [4096], P('mp')
- new_centroids: bfloat16 [4096, 3584], P('mp', 'dp')
The draws below stay inside these ranges and needn't reach their ends.
All inputs are finite; a program needn't handle non-finite values.
Results may differ from the reference program's by a relative error of at most 0.0011.
Values may be sent and summed in bfloat16 or wider, within the bound.
A program may use at most 64 MiB of HBM per device.

```python
import jax
import jax.numpy as jnp
from jax import lax

D = 3584
K = 4096
DOCS = 2048


def weight_matrix(key):
    bound_value = 0.99 * (3.0 / D) ** 0.5
    return jax.random.uniform(jax.random.fold_in(key, 101), (D, D), jnp.float32, -bound_value, bound_value)


def pooled_common(key):
    bound_value = 3.0 ** 0.5
    return jax.random.uniform(jax.random.fold_in(key, 102), (D,), jnp.float32, -bound_value, bound_value)


def embedded_common(key):
    projected = jnp.dot(pooled_common(key), weight_matrix(key), precision=lax.Precision.HIGHEST)
    return projected / jnp.sqrt(jnp.sum(projected * projected))


def count_values(key):
    return jnp.exp(jax.random.uniform(jax.random.fold_in(key, 103), (K,), jnp.float32, 0.0, jnp.log(8.0)))


def draw_w_out(key, part):
    return weight_matrix(key).astype(jnp.bfloat16)


def draw_pooled(key, part):
    noise_key = jax.random.fold_in(key, 104)
    loading_key = jax.random.fold_in(key, 105)
    noise_part = jax.random.normal(noise_key, (DOCS, D), jnp.float32)
    loadings = jax.random.uniform(loading_key, (DOCS, 1), jnp.float32, -1.5, 1.5)
    drawn_values = jnp.clip(noise_part + loadings * pooled_common(key)[None, :], -4.0, 4.0)
    return drawn_values.astype(jnp.bfloat16)


def draw_ema_counts(key, part):
    return count_values(key)


def draw_ema_sums(key, part):
    member_counts = count_values(key)
    shared_dir = embedded_common(key)
    random_part = jax.random.normal(jax.random.fold_in(key, 106), (K, D), jnp.float32)
    along_shared = jnp.sum(random_part * shared_dir[None, :], axis=1, keepdims=True)
    random_part = random_part - along_shared * shared_dir[None, :]
    random_part = random_part / jnp.sqrt(jnp.sum(random_part * random_part, axis=1, keepdims=True))
    alignment = jax.random.uniform(jax.random.fold_in(key, 107), (K, 1), jnp.float32, -0.9, 0.9)
    radius = jax.random.uniform(jax.random.fold_in(key, 108), (K, 1), jnp.float32, 0.3, 1.0)
    direction = radius * (alignment * shared_dir[None, :] + jnp.sqrt(1.0 - alignment * alignment) * random_part)
    bound_value = 24.0 * D ** (-0.5)
    return jnp.clip(member_counts[:, None] * direction, -bound_value, bound_value)


def place_ends(drawn, stream_key, least, largest):
    dims = drawn.shape
    index_at = [jax.random.randint(jax.random.fold_in(stream_key, axis), (), 0, dims[axis]) for axis in range(len(dims))]
    drawn = drawn.at[tuple(index_at)].set(least)
    longest = dims.index(max(dims))
    index_at[longest] = (index_at[longest] + 1) % dims[longest]
    return drawn.at[tuple(index_at)].set(largest)


def setup_inputs(seed: int = 0) -> dict:
    key_list = jax.random.split(jax.random.key(seed), 6)
    return {
        "pooled": draw_pooled(jax.random.fold_in(key_list[5], 71), 0),
        "w_out": draw_w_out(jax.random.fold_in(key_list[5], 71), 0),
        "assignments": place_ends(jax.random.randint(key_list[2], (DOCS,), 0, K), jax.random.fold_in(key_list[2], 1), 0, K - 1).astype(jnp.int32),
        "ema_sums": draw_ema_sums(jax.random.fold_in(key_list[5], 71), 0),
        "ema_counts": draw_ema_counts(jax.random.fold_in(key_list[5], 71), 0),
    }


def reference(pooled, w_out, assignments, ema_sums, ema_counts):
    proj = jnp.dot(pooled, w_out, preferred_element_type=jnp.float32)
    inverse_norm = 1.0 / jnp.sqrt(lax.optimization_barrier(jnp.sum(proj * proj, axis=1, keepdims=True)) + 1e-06)
    embedded = (proj * inverse_norm).astype(jnp.bfloat16)
    centers = (ema_sums / ema_counts[:, None]).astype(jnp.bfloat16)
    embed_wide = embedded.astype(jnp.float32)
    center_wide = centers.astype(jnp.float32)
    doc_norms = lax.optimization_barrier(jnp.sum(embed_wide * embed_wide, axis=1))
    center_norms = lax.optimization_barrier(jnp.sum(center_wide * center_wide, axis=1))
    products = jnp.dot(embedded, centers.T, preferred_element_type=jnp.float32)
    distances = doc_norms[:, None] + center_norms[None, :] - 2.0 * products
    batch_sums = jax.ops.segment_sum(embed_wide, assignments, num_segments=K)
    batch_counts = jax.ops.segment_sum(jnp.ones(assignments.shape, jnp.float32), assignments, num_segments=K)
    new_counts = 0.9 * ema_counts + 0.1 * batch_counts
    new_sums = 0.9 * ema_sums + 0.1 * batch_sums
    new_centroids = (new_sums / new_counts[:, None]).astype(jnp.bfloat16)
    return (distances, new_sums, new_counts, new_centroids)
```

```python
import functools
import math

import jax
import jax.numpy as jnp
from jax import lax
from jax.experimental import pallas as pl
from jax.experimental.pallas import tpu as pltpu
from jax.sharding import PartitionSpec as P

EPSILON = 1e-06
EMA_DECAY = 0.9
BF = jnp.bfloat16
F32 = jnp.float32
ORDER = (0, 2, 1, 3)


def plain_body(pooled, w_out, assignments, ema_sums, ema_counts):
    partial_value = jnp.dot(pooled, w_out, preferred_element_type=F32)
    projected = lax.psum(partial_value, "mp")
    inverse_norm = 1.0 / jnp.sqrt(jnp.sum(projected * projected, axis=1, keepdims=True) + EPSILON)
    embedded = (projected * inverse_norm).astype(BF)
    local_centers = ema_sums.shape[0]
    doc_rows = embedded.shape[0]
    centers = (ema_sums / ema_counts[:, None]).astype(BF)
    column_piece = lax.all_gather(centers, "dp", axis=1, tiled=True)
    products = lax.dot_general(
        embedded, column_piece, (((1,), (1,)), ((), ())), preferred_element_type=F32
    )
    piece_wide = column_piece.astype(F32)
    center_norms = jnp.sum(piece_wide * piece_wide, axis=1)
    embed_wide = embedded.astype(F32)
    doc_norms = jnp.sum(embed_wide * embed_wide, axis=1)
    distances = doc_norms[:, None] + center_norms[None, :] - 2.0 * products
    first_center = lax.axis_index("mp") * local_centers
    center_ids = first_center + jnp.arange(local_centers, dtype=jnp.int32)
    feature_cols = ema_sums.shape[1]
    every_assign = lax.all_gather(assignments, "dp", axis=0, tiled=True)
    own_columns = lax.all_to_all(embedded, "dp", split_axis=1, concat_axis=0, tiled=True)
    shard_count = lax.axis_size("dp")
    group_size = math.gcd(shard_count, max(1, 2048 // doc_rows))
    block_rows = group_size * doc_rows
    turns = shard_count // group_size

    def add_block(block_index, totals):
        sums_now, counts_now = totals
        block_assign = lax.dynamic_slice_in_dim(every_assign, block_index * block_rows, block_rows, 0)
        block_columns = lax.dynamic_slice_in_dim(own_columns, block_index * block_rows, block_rows, 0)
        one_hot = (block_assign[None, :] == center_ids[:, None]).astype(BF)
        sums_now = sums_now + jnp.dot(one_hot, block_columns, preferred_element_type=F32)
        counts_now = counts_now + jnp.sum(one_hot, axis=1, dtype=F32)
        return (sums_now, counts_now)

    start_sums = (jnp.zeros((local_centers, feature_cols), F32), jnp.zeros((local_centers,), F32))
    batch_sums, batch_counts = lax.fori_loop(0, turns, add_block, start_sums)
    return finish(distances, batch_sums, batch_counts, ema_sums, ema_counts)


def finish(distances, batch_sums, batch_counts, ema_sums, ema_counts):
    new_counts = EMA_DECAY * ema_counts + (1.0 - EMA_DECAY) * batch_counts
    new_sums = EMA_DECAY * ema_sums + (1.0 - EMA_DECAY) * batch_sums
    new_centroids = (new_sums / new_counts[:, None]).astype(BF)
    return (distances, new_sums, new_counts, new_centroids)


def kernel(
    pooled_ref, w_hbm, cent_own, asg_own,
    dist_ref, sums_ref, counts_ref,
    w_ref, pf, send_far, send_near, relay, finals, embf, own, cent, asg, onehot,
    w_sem, cs, cr, as_, ar, zs, zr, fs, fr, gs, gr, es, er,
):
    d = lax.axis_index("dp")
    m = lax.axis_index("mp")
    docs = pooled_ref.shape[0]
    quarter = docs // 4
    dim = w_ref.shape[1]
    chunk = dim // 4
    feats, centers = cent_own.shape
    half = feats // 2
    core, xi, yi = d % 2, (d // 2) % 2, d // 4

    def partner(k):
        return ((yi + k // 4) % 2) * 4 + ((xi + (k // 2) % 2) % 2) * 2 + (core + k % 2) % 2

    right, left, far = (m + 1) % 4, (m + 3) % 4, (m + 2) % 4
    PC, XN, YN, DG = partner(1), partner(2), partner(4), partner(6)

    def remote(src, dst, ssem, rsem, dp, mp):
        return pltpu.make_async_remote_copy(
            src_ref=src, dst_ref=dst, send_sem=ssem, recv_sem=rsem,
            device_id={"dp": dp, "mp": mp}, device_id_type=pl.DeviceIdType.MESH,
        )

    def cols(c):
        return pl.ds(c * chunk, chunk)

    def rows(q):
        return pl.ds(pl.multiple_of(q * quarter, quarter), quarter)

    w_copies = {}
    for c in ORDER:
        w_copies[c] = pltpu.make_async_copy(w_hbm.at[:, cols(c)], w_ref.at[:, cols(c)], w_sem.at[c])
        w_copies[c].start()

    barrier = pltpu.get_barrier_semaphore()
    for k in range(1, 8):
        pl.semaphore_signal(barrier, inc=1, device_id={"dp": partner(k), "mp": m}, device_id_type=pl.DeviceIdType.MESH)
    for z in (right, left):
        pl.semaphore_signal(barrier, inc=1, device_id={"dp": d, "mp": z}, device_id_type=pl.DeviceIdType.MESH)
    pl.semaphore_wait(barrier, 9)

    def slot(b):
        return cent.at[pl.ds(pl.multiple_of(b * feats, feats), feats), :]

    def half_slot(b, h):
        return cent.at[pl.ds(pl.multiple_of(b * feats + h * half, half), half), :]

    sends = []

    def go(copy):
        copy.start()
        sends.append(copy)
        return copy

    asg_copies = {}
    for k in range(1, 8):
        asg_copies[k] = go(remote(asg_own, asg.at[d], as_.at[k], ar.at[k], partner(k), m))
    c_x = go(remote(cent_own, slot(d), cs.at[0], cr.at[0], XN, m))
    c_y = go(remote(cent_own, slot(d), cs.at[1], cr.at[1], YN, m))
    c_p = go(remote(cent_own, slot(d), cs.at[2], cr.at[2], PC, m))

    z_copies = {}
    for c in ORDER:
        w_copies[c].wait()
        pf[:, cols(c)] = jnp.dot(pooled_ref[...], w_ref[:, cols(c)], preferred_element_type=F32)
        send_far[:, cols(c)] = pf[rows(far), cols(c)].astype(BF)
        z_copies[c] = go(remote(
            send_far.at[:, cols(c)], relay.at[:, cols(c)], zs.at[c], zr.at[c], d, right if c < 2 else left))
        side = 1 if c < 2 else 0
        to = left if c < 2 else right
        send_near[side, :, cols(c)] = pf[rows(to), cols(c)].astype(BF)
        z_copies[(side, c)] = go(remote(
            send_near.at[side, :, cols(c)], finals.at[side, :, cols(c)], fs.at[side, c], fr.at[side, c], d, to))
    for c in ORDER:
        z_copies[c].wait_recv()
        side = 0 if c < 2 else 1
        to = right if c < 2 else left
        send_near[side, :, cols(c)] = (pf[rows(to), cols(c)] + relay[:, cols(c)].astype(F32)).astype(BF)
        z_copies[(side, c)] = go(remote(
            send_near.at[side, :, cols(c)], finals.at[side, :, cols(c)], fs.at[side, c], fr.at[side, c], d, to))

    first_center = m * centers
    ids = first_center + lax.broadcasted_iota(jnp.int32, (centers, docs), 0)
    counts = jnp.zeros((8, centers), F32)
    for k in range(8):
        if k:
            asg_copies[k].wait_recv()
            row = asg[partner(k)][0:1, :]
        else:
            row = asg_own[0:1, :]
        onehot[k] = jnp.where(ids == row, 1.0, 0.0).astype(BF)
        counts = counts + lax.dot_general(
            jnp.ones((8, docs), BF), onehot[k], (((1,), (1,)), ((), ())), preferred_element_type=F32)
    counts_ref[...] = counts

    total = jnp.zeros((quarter, 1), F32)
    for c in ORDER:
        for side in (0, 1):
            z_copies[(side, c)].wait_recv()
        part = pf[rows(m), cols(c)] + finals[0, :, cols(c)].astype(F32) + finals[1, :, cols(c)].astype(F32)
        pf[rows(m), cols(c)] = part
        total = total + jnp.sum(part * part, axis=1, keepdims=True)
    inverse = 1.0 / jnp.sqrt(total + EPSILON)
    mine = pf[rows(m), :] * inverse
    for b in range(8):
        embf[b, rows(m), :] = mine[:, b * feats:(b + 1) * feats].astype(BF)

    def emb(q, lo):
        return embf.at[pl.ds(lo, 4), rows(q), :]

    g_copies = {}
    for step in (0, 1):
        for side, to in ((0, right), (1, left)):
            lo = 4 * ((step + side) % 2)
            g_copies[(side, step)] = go(remote(emb(m, lo), emb(m, lo), gs.at[side, step], gr.at[side, step], d, to))

    e_copies = {}

    def scatter(r):
        q = (m + r) % 4
        for k in (1, 2, 4, 6, 3, 5, 7):
            e_copies[(r, k)] = go(remote(
                embf.at[partner(k), rows(q), :], own.at[d, rows(q), :], es.at[r, k], er.at[r, k], partner(k), m))

    c_x.wait_recv()
    c_rx = go(remote(half_slot(XN, 0), half_slot(XN, 0), cs.at[3], cr.at[3], YN, m))
    c_px = go(remote(slot(XN), slot(XN), cs.at[5], cr.at[5], PC, m))
    c_y.wait_recv()
    c_ry = go(remote(half_slot(YN, 1), half_slot(YN, 1), cs.at[4], cr.at[4], XN, m))
    c_py = go(remote(slot(YN), slot(YN), cs.at[6], cr.at[6], PC, m))
    scatter(0)

    g_copies[(0, 0)].wait_recv()
    g_copies[(0, 2)] = go(remote(emb(left, 0), emb(left, 0), gs.at[0, 2], gr.at[0, 2], d, right))
    g_copies[(1, 0)].wait_recv()
    g_copies[(1, 2)] = go(remote(emb(right, 4), emb(right, 4), gs.at[1, 2], gr.at[1, 2], d, left))
    g_copies[(0, 1)].wait_recv()
    scatter(3)
    g_copies[(1, 1)].wait_recv()
    scatter(1)
    c_rx.wait_recv()
    c_pd0 = go(remote(half_slot(DG, 0), half_slot(DG, 0), cs.at[7], cr.at[7], PC, m))
    c_ry.wait_recv()
    c_pd1 = go(remote(half_slot(DG, 1), half_slot(DG, 1), cs.at[8], cr.at[8], PC, m))
    g_copies[(0, 2)].wait_recv()
    g_copies[(1, 2)].wait_recv()
    scatter(2)

    doc_norms = jnp.zeros((docs, 1), F32)
    for b in range(8):
        wide = embf[b].astype(F32)
        doc_norms = doc_norms + jnp.sum(wide * wide, axis=1, keepdims=True)
    norms = jnp.zeros((1, centers), F32)
    waits = {1: (c_p,), 3: (c_px,), 5: (c_py,), 7: (c_pd0, c_pd1)}
    for k in (0, 2, 4, 6, 1, 3, 5, 7):
        for copy in waits.get(k, ()):
            copy.wait_recv()
        block = slot(partner(k))[...] if k else cent_own[...]
        wide = block.astype(F32)
        norms = norms + jnp.sum(wide * wide, axis=0, keepdims=True)
        product = jnp.dot(embf[partner(k)], block, preferred_element_type=F32)
        if k == 0:
            dist_ref[...] = product
        elif k < 7:
            dist_ref[...] += product
        else:
            dist_ref[...] = doc_norms + norms - 2.0 * (dist_ref[...] + product)

    sums_ref[...] = jnp.dot(onehot[0], embf[d], preferred_element_type=F32)
    for k in (1, 2, 4, 6, 3, 5, 7):
        for r in range(4):
            e_copies[(r, k)].wait_recv()
        sums_ref[...] += jnp.dot(onehot[k], own[partner(k)], preferred_element_type=F32)
    for copy in sends:
        copy.wait_send()


def fast_body(pooled, w_out, assignments, ema_sums, ema_counts):
    docs, depth = pooled.shape
    dim = w_out.shape[1]
    centers, feats = ema_sums.shape
    quarter = docs // 4
    cent = (ema_sums / ema_counts[:, None]).astype(BF).T
    asg8 = jnp.broadcast_to(assignments[None, :], (8, docs))
    vmem = pl.BlockSpec(memory_space=pltpu.VMEM)
    dma = pltpu.SemaphoreType.DMA
    distances, batch_sums, counts = pl.pallas_call(
        kernel,
        out_shape=(
            jax.ShapeDtypeStruct((docs, centers), F32),
            jax.ShapeDtypeStruct((centers, feats), F32),
            jax.ShapeDtypeStruct((8, centers), F32),
        ),
        in_specs=[vmem, pl.BlockSpec(memory_space=pl.ANY), vmem, vmem],
        out_specs=(vmem, vmem, vmem),
        scratch_shapes=[
            pltpu.VMEM((depth, dim), BF),
            pltpu.VMEM((docs, dim), F32),
            pltpu.VMEM((quarter, dim), BF),
            pltpu.VMEM((2, quarter, dim), BF),
            pltpu.VMEM((quarter, dim), BF),
            pltpu.VMEM((2, quarter, dim), BF),
            pltpu.VMEM((8, docs, feats), BF),
            pltpu.VMEM((8, docs, feats), BF),
            pltpu.VMEM((8 * feats, centers), BF),
            pltpu.VMEM((8, 8, docs), jnp.int32),
            pltpu.VMEM((8, centers, docs), BF),
            dma((4,)), dma((9,)), dma((9,)), dma((8,)), dma((8,)), dma((4,)), dma((4,)),
            dma((2, 4)), dma((2, 4)), dma((2, 3)), dma((2, 3)), dma((4, 8)), dma((4, 8)),
        ],
        compiler_params=pltpu.CompilerParams(
            collective_id=0, has_side_effects=True, vmem_limit_bytes=60 * 1024 * 1024),
        name="embed_and_assign",
    )(pooled, w_out, cent, asg8)
    return finish(distances, batch_sums, counts[0], ema_sums, ema_counts)


def solution(mesh):
    fast = mesh.shape["dp"] == 8 and mesh.shape["mp"] == 4
    return jax.shard_map(
        fast_body if fast else plain_body,
        mesh=mesh,
        in_specs=(P("dp", "mp"), P("mp", None), P("dp"), P("mp", "dp"), P("mp")),
        out_specs=(P("dp", "mp"), P("mp", "dp"), P("mp"), P("mp", "dp")),
        check_vma=False,
    )
```

```python
import functools
import math

import jax
import jax.numpy as jnp
from jax import lax
from jax.experimental import pallas as pl
from jax.experimental.pallas import tpu as pltpu
from jax.sharding import PartitionSpec as P

EPSILON = 1e-06
EMA_DECAY = 0.9
BF = jnp.bfloat16
F32 = jnp.float32


def plain_body(pooled, w_out, assignments, ema_sums, ema_counts):
    partial_value = jnp.dot(pooled, w_out, preferred_element_type=F32)
    projected = lax.psum(partial_value, "mp")
    inverse_norm = 1.0 / jnp.sqrt(jnp.sum(projected * projected, axis=1, keepdims=True) + EPSILON)
    embedded = (projected * inverse_norm).astype(BF)
    local_centers = ema_sums.shape[0]
    doc_rows = embedded.shape[0]
    centers = (ema_sums / ema_counts[:, None]).astype(BF)
    column_piece = lax.all_gather(centers, "dp", axis=1, tiled=True)
    products = lax.dot_general(
        embedded, column_piece, (((1,), (1,)), ((), ())), preferred_element_type=F32
    )
    piece_wide = column_piece.astype(F32)
    center_norms = jnp.sum(piece_wide * piece_wide, axis=1)
    embed_wide = embedded.astype(F32)
    doc_norms = jnp.sum(embed_wide * embed_wide, axis=1)
    distances = doc_norms[:, None] + center_norms[None, :] - 2.0 * products
    first_center = lax.axis_index("mp") * local_centers
    center_ids = first_center + jnp.arange(local_centers, dtype=jnp.int32)
    feature_cols = ema_sums.shape[1]
    every_assign = lax.all_gather(assignments, "dp", axis=0, tiled=True)
    own_columns = lax.all_to_all(embedded, "dp", split_axis=1, concat_axis=0, tiled=True)
    shard_count = lax.axis_size("dp")
    group_size = math.gcd(shard_count, max(1, 2048 // doc_rows))
    block_rows = group_size * doc_rows
    turns = shard_count // group_size

    def add_block(block_index, totals):
        sums_now, counts_now = totals
        block_assign = lax.dynamic_slice_in_dim(every_assign, block_index * block_rows, block_rows, 0)
        block_columns = lax.dynamic_slice_in_dim(own_columns, block_index * block_rows, block_rows, 0)
        one_hot = (block_assign[None, :] == center_ids[:, None]).astype(BF)
        sums_now = sums_now + jnp.dot(one_hot, block_columns, preferred_element_type=F32)
        counts_now = counts_now + jnp.sum(one_hot, axis=1, dtype=F32)
        return (sums_now, counts_now)

    start_sums = (jnp.zeros((local_centers, feature_cols), F32), jnp.zeros((local_centers,), F32))
    batch_sums, batch_counts = lax.fori_loop(0, turns, add_block, start_sums)
    return finish(distances, batch_sums, batch_counts, ema_sums, ema_counts)


def finish(distances, batch_sums, batch_counts, ema_sums, ema_counts):
    new_counts = EMA_DECAY * ema_counts + (1.0 - EMA_DECAY) * batch_counts
    new_sums = EMA_DECAY * ema_sums + (1.0 - EMA_DECAY) * batch_sums
    new_centroids = (new_sums / new_counts[:, None]).astype(BF)
    return (distances, new_sums, new_counts, new_centroids)


def kernel(
    pooled_ref, w_hbm, cent_own, asg_own,
    dist_ref, sums_ref, counts_ref,
    w_ref, pf, outgoing, incoming, embf, own, cent, asg, onehot,
    w_sem, cs, cr, as_, ar, zs, zr, gs, gr, es, er,
):
    d = lax.axis_index("dp")
    m = lax.axis_index("mp")
    docs = pooled_ref.shape[0]
    quarter = docs // 4
    dim = w_ref.shape[1]
    chunk = dim // 4
    feats, centers = cent_own.shape
    half = feats // 2
    core, xi, yi = d % 2, (d // 2) % 2, d // 4

    def partner(k):
        return ((yi + k // 4) % 2) * 4 + ((xi + (k // 2) % 2) % 2) * 2 + (core + k % 2) % 2

    near = m // 2
    far = 1 - near
    inner = (m + near) % 2
    ahead = m + 1 - 2 * near
    behind = m - inner * (1 - 2 * near) + (1 - inner) * (1 - 2 * near)
    PC, XN, YN, DG = partner(1), partner(2), partner(4), partner(6)

    def remote(src, dst, ssem, rsem, dp, mp):
        return pltpu.make_async_remote_copy(
            src_ref=src, dst_ref=dst, send_sem=ssem, recv_sem=rsem,
            device_id={"dp": dp, "mp": mp}, device_id_type=pl.DeviceIdType.MESH,
        )

    def cols(c):
        return pl.ds(c * chunk, chunk)

    def rows(flow, i):
        return pl.ds(pl.multiple_of((flow * 2 + i) * quarter, quarter), quarter)

    w_copies = []
    for c in range(4):
        w_copies.append(pltpu.make_async_copy(w_hbm.at[:, cols(c)], w_ref.at[:, cols(c)], w_sem.at[c]))
        w_copies[c].start()

    barrier = pltpu.get_barrier_semaphore()
    for k in range(1, 8):
        pl.semaphore_signal(barrier, inc=1, device_id={"dp": partner(k), "mp": m}, device_id_type=pl.DeviceIdType.MESH)
    pl.semaphore_signal(barrier, inc=1, device_id={"dp": d, "mp": ahead}, device_id_type=pl.DeviceIdType.MESH)

    @pl.when(inner == 1)
    def _():
        pl.semaphore_signal(barrier, inc=1, device_id={"dp": d, "mp": behind}, device_id_type=pl.DeviceIdType.MESH)

    pl.semaphore_wait(barrier, 8 + inner)

    def slot(b):
        return cent.at[pl.ds(pl.multiple_of(b * feats, feats), feats), :]

    def half_slot(b, h):
        return cent.at[pl.ds(pl.multiple_of(b * feats + h * half, half), half), :]

    def half_own(h):
        return cent_own.at[pl.ds(h * half, half), :]

    sends = []

    def go(copy):
        copy.start()
        sends.append(copy)
        return copy

    c_x, c_y = {}, {}
    for h in (0, 1):
        c_x[h] = go(remote(half_own(h), half_slot(d, h), cs.at[h], cr.at[h], XN, m))
        g = 1 - h
        c_y[g] = go(remote(half_own(g), half_slot(d, g), cs.at[2 + g], cr.at[2 + g], YN, m))
    c_p = go(remote(cent_own, slot(d), cs.at[4], cr.at[4], PC, m))
    asg_copies = {}
    for k in range(1, 8):
        asg_copies[k] = go(remote(asg_own, asg.at[d], as_.at[k], ar.at[k], partner(k), m))

    def sum_copy(flow, i, c, to):
        at = (flow, pl.ds(i * quarter, quarter), cols(c))
        return remote(outgoing.at[at], incoming.at[at], zs.at[flow, i, c], zr.at[flow, i, c], d, to)

    def put(flow, i, c, value):
        outgoing[flow, pl.ds(i * quarter, quarter), cols(c)] = value.astype(BF)

    def arrived(flow, i, c):
        return pf[rows(flow, i), cols(c)] + incoming[flow, pl.ds(i * quarter, quarter), cols(c)].astype(F32)

    for c in range(4):
        w_copies[c].wait()
        pf[:, cols(c)] = jnp.dot(pooled_ref[...], w_ref[:, cols(c)], preferred_element_type=F32)

        @pl.when(inner == 0)
        def _():
            put(near, 0, c, pf[rows(near, 0), cols(c)])
            sum_copy(near, 0, c, ahead).start()

    @pl.when(inner == 0)
    def _():
        for c in range(4):
            put(near, 1, c, pf[rows(near, 1), cols(c)])
            sum_copy(near, 1, c, ahead).start()

    def sum_near(i, c):
        @pl.when(inner == 1)
        def _():
            sum_copy(near, i, c, ahead).wait_recv()
            put(near, i, c, arrived(near, i, c))
            sum_copy(near, i, c, ahead).start()

    def sum_far(i, c):
        sum_copy(far, i, c, behind).wait_recv()

        @pl.when(inner == 1)
        def _():
            put(far, i, c, arrived(far, i, c))
            sum_copy(far, i, c, behind).start()

        @pl.when(inner == 0)
        def _():
            pf[rows(far, i), cols(c)] = arrived(far, i, c)

    def emb_copy(flow, i, b, to):
        ref = embf.at[pl.ds(2 * b, 2), rows(flow, i), :]
        return remote(ref, ref, gs.at[flow, i, b], gr.at[flow, i, b], d, to)

    def embed(i):
        @pl.when(inner == 0)
        def _():
            value = pf[rows(far, i), :]
            inverse = 1.0 / jnp.sqrt(jnp.sum(value * value, axis=1, keepdims=True) + EPSILON)
            value = value * inverse
            for b in range(8):
                embf[b, rows(far, i), :] = value[:, b * feats:(b + 1) * feats].astype(BF)
            for b in range(4):
                emb_copy(far, i, b, ahead).start()

    def emb_near(i, b):
        @pl.when(inner == 1)
        def _():
            emb_copy(far, i, b, ahead).wait_recv()
            emb_copy(far, i, b, ahead).start()

    def emb_far(i, b):
        emb_copy(near, i, b, behind).wait_recv()

        @pl.when(inner == 1)
        def _():
            emb_copy(near, i, b, behind).start()

    e_copies = {}

    def scatter(name, flow, i):
        for k in (1, 2, 4, 6, 3, 5, 7):
            e_copies[(name, i, k)] = go(remote(
                embf.at[partner(k), rows(flow, i), :], own.at[d, rows(flow, i), :],
                es.at[flow, i, k], er.at[flow, i, k], partner(k), m))

    for t in range(5):
        if t < 4:
            sum_near(0, t)
        if t >= 1:
            sum_far(0, t - 1)
    embed(0)
    c_x[0].wait_recv()
    c_rx = go(remote(half_slot(XN, 0), half_slot(XN, 0), cs.at[5], cr.at[5], YN, m))
    c_y[1].wait_recv()
    c_ry = go(remote(half_slot(YN, 1), half_slot(YN, 1), cs.at[6], cr.at[6], XN, m))
    for t in range(7):
        if t < 4:
            sum_near(1, t)
        if 1 <= t < 5:
            sum_far(1, t - 1)
        if t == 4:
            embed(1)
        if 2 <= t < 6:
            emb_near(0, t - 2)
        if 3 <= t:
            emb_far(0, t - 3)
    scatter("far", far, 0)
    scatter("near", near, 0)
    c_x[1].wait_recv()
    c_px = go(remote(slot(XN), slot(XN), cs.at[7], cr.at[7], PC, m))
    c_y[0].wait_recv()
    c_py = go(remote(slot(YN), slot(YN), cs.at[8], cr.at[8], PC, m))
    for t in range(5):
        if t < 4:
            emb_near(1, t)
        if t >= 1:
            emb_far(1, t - 1)
    scatter("far", far, 1)
    scatter("near", near, 1)
    c_rx.wait_recv()
    c_pd0 = go(remote(half_slot(DG, 0), half_slot(DG, 0), cs.at[9], cr.at[9], PC, m))
    c_ry.wait_recv()
    c_pd1 = go(remote(half_slot(DG, 1), half_slot(DG, 1), cs.at[10], cr.at[10], PC, m))

    first_center = m * centers
    ids = first_center + lax.broadcasted_iota(jnp.int32, (centers, docs), 0)
    counts = jnp.zeros((8, centers), F32)
    for k in range(8):
        if k:
            asg_copies[k].wait_recv()
            row = asg[partner(k)][0:1, :]
        else:
            row = asg_own[0:1, :]
        onehot[k] = jnp.where(ids == row, 1.0, 0.0).astype(BF)
        counts = counts + lax.dot_general(
            jnp.ones((8, docs), BF), onehot[k], (((1,), (1,)), ((), ())), preferred_element_type=F32)
    counts_ref[...] = counts

    doc_norms = jnp.zeros((docs, 1), F32)
    for b in range(8):
        wide = embf[b].astype(F32)
        doc_norms = doc_norms + jnp.sum(wide * wide, axis=1, keepdims=True)
    norms = jnp.zeros((1, centers), F32)
    waits = {1: (c_p,), 3: (c_px,), 5: (c_py,), 7: (c_pd0, c_pd1)}
    for k in (0, 2, 4, 6, 1, 3, 5, 7):
        for copy in waits.get(k, ()):
            copy.wait_recv()
        block = slot(partner(k))[...] if k else cent_own[...]
        wide = block.astype(F32)
        norms = norms + jnp.sum(wide * wide, axis=0, keepdims=True)
        product = jnp.dot(embf[partner(k)], block, preferred_element_type=F32)
        if k == 0:
            dist_ref[...] = product
        elif k < 7:
            dist_ref[...] += product
        else:
            dist_ref[...] = doc_norms + norms - 2.0 * (dist_ref[...] + product)

    sums_ref[...] = jnp.dot(onehot[0], embf[d], preferred_element_type=F32)
    for k in (1, 2, 4, 6, 3, 5, 7):
        for i in range(2):
            for name in ("far", "near"):
                e_copies[(name, i, k)].wait_recv()
        sums_ref[...] += jnp.dot(onehot[k], own[partner(k)], preferred_element_type=F32)
    for copy in sends:
        copy.wait_send()
    for i in range(2):
        for c in range(4):
            sum_copy(near, i, c, ahead).wait_send()
            emb_copy(far, i, c, ahead).wait_send()

    @pl.when(inner == 1)
    def _():
        for i in range(2):
            for c in range(4):
                sum_copy(far, i, c, behind).wait_send()
                emb_copy(near, i, c, behind).wait_send()


def fast_body(pooled, w_out, assignments, ema_sums, ema_counts):
    docs, depth = pooled.shape
    dim = w_out.shape[1]
    centers, feats = ema_sums.shape
    cent = (ema_sums / ema_counts[:, None]).astype(BF).T
    asg8 = jnp.broadcast_to(assignments[None, :], (8, docs))
    vmem = pl.BlockSpec(memory_space=pltpu.VMEM)
    dma = pltpu.SemaphoreType.DMA
    distances, batch_sums, counts = pl.pallas_call(
        kernel,
        out_shape=(
            jax.ShapeDtypeStruct((docs, centers), F32),
            jax.ShapeDtypeStruct((centers, feats), F32),
            jax.ShapeDtypeStruct((8, centers), F32),
        ),
        in_specs=[vmem, pl.BlockSpec(memory_space=pl.ANY), vmem, vmem],
        out_specs=(vmem, vmem, vmem),
        scratch_shapes=[
            pltpu.VMEM((depth, dim), BF),
            pltpu.VMEM((docs, dim), F32),
            pltpu.VMEM((2, docs // 2, dim), BF),
            pltpu.VMEM((2, docs // 2, dim), BF),
            pltpu.VMEM((8, docs, feats), BF),
            pltpu.VMEM((8, docs, feats), BF),
            pltpu.VMEM((8 * feats, centers), BF),
            pltpu.VMEM((8, 8, docs), jnp.int32),
            pltpu.VMEM((8, centers, docs), BF),
            dma((4,)), dma((11,)), dma((11,)), dma((8,)), dma((8,)), dma((2, 2, 4)), dma((2, 2, 4)),
            dma((2, 2, 4)), dma((2, 2, 4)), dma((2, 2, 8)), dma((2, 2, 8)),
        ],
        compiler_params=pltpu.CompilerParams(
            collective_id=0, has_side_effects=True, vmem_limit_bytes=60 * 1024 * 1024),
        name="embed_and_assign",
    )(pooled, w_out, cent, asg8)
    return finish(distances, batch_sums, counts[0], ema_sums, ema_counts)


def solution(mesh):
    fast = mesh.shape["dp"] == 8 and mesh.shape["mp"] == 4
    return jax.shard_map(
        fast_body if fast else plain_body,
        mesh=mesh,
        in_specs=(P("dp", "mp"), P("mp", None), P("dp"), P("mp", "dp"), P("mp")),
        out_specs=(P("dp", "mp"), P("mp", "dp"), P("mp"), P("mp", "dp")),
        check_vma=False,
    )
```

```python
import functools
import math

import jax
import jax.numpy as jnp
from jax import lax
from jax.experimental import pallas as pl
from jax.experimental.pallas import tpu as pltpu
from jax.sharding import PartitionSpec as P

EPSILON = 1e-06
EMA_DECAY = 0.9
BF = jnp.bfloat16
F32 = jnp.float32
BLOCKS = 4
PIECES = 2


def plain_body(pooled, w_out, assignments, ema_sums, ema_counts):
    partial_value = jnp.dot(pooled, w_out, preferred_element_type=F32)
    projected = lax.psum(partial_value, "mp")
    inverse_norm = 1.0 / jnp.sqrt(jnp.sum(projected * projected, axis=1, keepdims=True) + EPSILON)
    embedded = (projected * inverse_norm).astype(BF)
    local_centers = ema_sums.shape[0]
    doc_rows = embedded.shape[0]
    centers = (ema_sums / ema_counts[:, None]).astype(BF)
    column_piece = lax.all_gather(centers, "dp", axis=1, tiled=True)
    products = lax.dot_general(
        embedded, column_piece, (((1,), (1,)), ((), ())), preferred_element_type=F32
    )
    piece_wide = column_piece.astype(F32)
    center_norms = jnp.sum(piece_wide * piece_wide, axis=1)
    embed_wide = embedded.astype(F32)
    doc_norms = jnp.sum(embed_wide * embed_wide, axis=1)
    distances = doc_norms[:, None] + center_norms[None, :] - 2.0 * products
    first_center = lax.axis_index("mp") * local_centers
    center_ids = first_center + jnp.arange(local_centers, dtype=jnp.int32)
    feature_cols = ema_sums.shape[1]
    every_assign = lax.all_gather(assignments, "dp", axis=0, tiled=True)
    own_columns = lax.all_to_all(embedded, "dp", split_axis=1, concat_axis=0, tiled=True)
    shard_count = lax.axis_size("dp")
    group_size = math.gcd(shard_count, max(1, 2048 // doc_rows))
    block_rows = group_size * doc_rows
    turns = shard_count // group_size

    def add_block(block_index, totals):
        sums_now, counts_now = totals
        block_assign = lax.dynamic_slice_in_dim(every_assign, block_index * block_rows, block_rows, 0)
        block_columns = lax.dynamic_slice_in_dim(own_columns, block_index * block_rows, block_rows, 0)
        one_hot = (block_assign[None, :] == center_ids[:, None]).astype(BF)
        sums_now = sums_now + jnp.dot(one_hot, block_columns, preferred_element_type=F32)
        counts_now = counts_now + jnp.sum(one_hot, axis=1, dtype=F32)
        return (sums_now, counts_now)

    start_sums = (jnp.zeros((local_centers, feature_cols), F32), jnp.zeros((local_centers,), F32))
    batch_sums, batch_counts = lax.fori_loop(0, turns, add_block, start_sums)
    return finish(distances, batch_sums, batch_counts, ema_sums, ema_counts)


def finish(distances, batch_sums, batch_counts, ema_sums, ema_counts):
    new_counts = EMA_DECAY * ema_counts + (1.0 - EMA_DECAY) * batch_counts
    new_sums = EMA_DECAY * ema_sums + (1.0 - EMA_DECAY) * batch_sums
    new_centroids = (new_sums / new_counts[:, None]).astype(BF)
    return (distances, new_sums, new_counts, new_centroids)


def kernel(
    pooled_ref, w_hbm, ema_ref, ema_counts_ref, asg_own,
    dist_ref, sums_ref, counts_ref,
    cent_own, w_ref, pf, outgoing, incoming, embf, own, cent, asg, onehot,
    w_sem, cs, cr, as_, ar, zs, zr, gs, gr, es, er,
):
    d = lax.axis_index("dp")
    m = lax.axis_index("mp")
    docs = pooled_ref.shape[0]
    block = docs // (2 * BLOCKS)
    dim = w_ref.shape[1]
    chunk = dim // 4
    wide = dim // PIECES
    heads = 8 // PIECES
    feats, centers = cent_own.shape
    half = feats // 2
    core, xi, yi = d % 2, (d // 2) % 2, d // 4

    def partner(k):
        return ((yi + k // 4) % 2) * 4 + ((xi + (k // 2) % 2) % 2) * 2 + (core + k % 2) % 2

    near = m // 2
    far = 1 - near
    inner = (m + near) % 2
    ahead = m + 1 - 2 * near
    behind = m - inner * (1 - 2 * near) + (1 - inner) * (1 - 2 * near)
    PC, XN, YN, DG = partner(1), partner(2), partner(4), partner(6)

    def remote(src, dst, ssem, rsem, dp, mp):
        return pltpu.make_async_remote_copy(
            src_ref=src, dst_ref=dst, send_sem=ssem, recv_sem=rsem,
            device_id={"dp": dp, "mp": mp}, device_id_type=pl.DeviceIdType.MESH,
        )

    def cols(c):
        return pl.ds(c * chunk, chunk)

    def pieces(c):
        return pl.ds(c * wide, wide)

    def rows(flow, i):
        return pl.ds(pl.multiple_of((i * 2 + flow) * block, block), block)

    w_copies = []
    for c in range(4):
        w_copies.append(pltpu.make_async_copy(w_hbm.at[:, cols(c)], w_ref.at[:, cols(c)], w_sem.at[c]))
        w_copies[c].start()
    cent_own[...] = (ema_ref[...] / ema_counts_ref[0:1, :]).astype(BF)

    barrier = pltpu.get_barrier_semaphore()
    for k in range(1, 8):
        pl.semaphore_signal(barrier, inc=1, device_id={"dp": partner(k), "mp": m}, device_id_type=pl.DeviceIdType.MESH)
    pl.semaphore_signal(barrier, inc=1, device_id={"dp": d, "mp": ahead}, device_id_type=pl.DeviceIdType.MESH)

    @pl.when(inner == 1)
    def _():
        pl.semaphore_signal(barrier, inc=1, device_id={"dp": d, "mp": behind}, device_id_type=pl.DeviceIdType.MESH)

    pl.semaphore_wait(barrier, 8 + inner)

    def slot(b):
        return cent.at[pl.ds(pl.multiple_of(b * feats, feats), feats), :]

    def half_slot(b, h):
        return cent.at[pl.ds(pl.multiple_of(b * feats + h * half, half), half), :]

    def half_own(h):
        return cent_own.at[pl.ds(h * half, half), :]

    sends = []

    def go(copy):
        copy.start()
        sends.append(copy)
        return copy

    c_x, c_y = {}, {}
    for h in (0, 1):
        c_x[h] = go(remote(half_own(h), half_slot(d, h), cs.at[h], cr.at[h], XN, m))
        g = 1 - h
        c_y[g] = go(remote(half_own(g), half_slot(d, g), cs.at[2 + g], cr.at[2 + g], YN, m))
    c_p = go(remote(cent_own, slot(d), cs.at[4], cr.at[4], PC, m))
    asg_copies = {}
    for k in range(1, 8):
        asg_copies[k] = go(remote(asg_own, asg.at[d], as_.at[k], ar.at[k], partner(k), m))

    def sum_copy(flow, i, c, to):
        at = (flow, pl.ds(i * block, block), pieces(c))
        return remote(outgoing.at[at], incoming.at[at], zs.at[flow, i, c], zr.at[flow, i, c], d, to)

    def put(flow, i, c, value):
        outgoing[flow, pl.ds(i * block, block), pieces(c)] = value.astype(BF)

    def arrived(flow, i, c):
        return pf[rows(flow, i), pieces(c)] + incoming[flow, pl.ds(i * block, block), pieces(c)].astype(F32)

    def begin(i, c):
        @pl.when(inner == 0)
        def _():
            put(near, i, c, pf[rows(near, i), pieces(c)])
            sum_copy(near, i, c, ahead).start()

    for c in range(4):
        w_copies[c].wait()
        pf[:, cols(c)] = jnp.dot(pooled_ref[...], w_ref[:, cols(c)], preferred_element_type=F32)
        if (c + 1) % (4 // PIECES) == 0:
            begin(0, c // (4 // PIECES))
    for i in range(1, BLOCKS):
        for c in range(PIECES):
            begin(i, c)

    def sum_near(i, c):
        @pl.when(inner == 1)
        def _():
            sum_copy(near, i, c, ahead).wait_recv()
            put(near, i, c, arrived(near, i, c))
            sum_copy(near, i, c, ahead).start()

    def sum_far(i, c):
        sum_copy(far, i, c, behind).wait_recv()

        @pl.when(inner == 1)
        def _():
            put(far, i, c, arrived(far, i, c))
            sum_copy(far, i, c, behind).start()

        @pl.when(inner == 0)
        def _():
            pf[rows(far, i), pieces(c)] = arrived(far, i, c)

    def emb_copy(flow, i, b, to):
        ref = embf.at[pl.ds(heads * b, heads), rows(flow, i), :]
        return remote(ref, ref, gs.at[flow, i, b], gr.at[flow, i, b], d, to)

    def embed(i):
        @pl.when(inner == 0)
        def _():
            value = pf[rows(far, i), :]
            inverse = 1.0 / jnp.sqrt(jnp.sum(value * value, axis=1, keepdims=True) + EPSILON)
            value = value * inverse
            for b in range(8):
                embf[b, rows(far, i), :] = value[:, b * feats:(b + 1) * feats].astype(BF)
            for b in range(PIECES):
                emb_copy(far, i, b, ahead).start()

    def emb_near(i, b):
        @pl.when(inner == 1)
        def _():
            emb_copy(far, i, b, ahead).wait_recv()
            emb_copy(far, i, b, ahead).start()

    def emb_far(i, b):
        emb_copy(near, i, b, behind).wait_recv()

        @pl.when(inner == 1)
        def _():
            emb_copy(near, i, b, behind).start()

    e_copies = {}

    def scatter(name, flow, i):
        for k in (1, 2, 4, 6, 3, 5, 7):
            e_copies[(name, i, k)] = go(remote(
                embf.at[partner(k), rows(flow, i), :], own.at[d, rows(flow, i), :],
                es.at[flow, i, k], er.at[flow, i, k], partner(k), m))

    def mark(k):
        if k:
            asg_copies[k].wait_recv()
            row = asg[partner(k)][0:1, :]
        else:
            row = asg_own[0:1, :]
        column = jnp.broadcast_to(row, (128, docs)).T
        for j in range(centers // 128):
            ids = m * centers + j * 128 + lax.broadcasted_iota(jnp.int32, (docs, 128), 1)
            onehot[k, :, j * 128:(j + 1) * 128] = jnp.where(ids == column, 1.0, 0.0).astype(BF)
        count = jnp.dot(jnp.ones((8, docs), BF), onehot[k], preferred_element_type=F32)
        counts_ref[...] = counts_ref[...] + count if k else count

    norms = []
    waits = {1: lambda: (c_p,), 3: lambda: (c_px,), 5: lambda: (c_py,), 7: lambda: (c_pd0, c_pd1)}

    def product(h, k):
        if h == 0 and k in waits:
            for copy in waits[k]():
                copy.wait_recv()
        piece = slot(partner(k))[...] if k else cent_own[...]
        if h == 0:
            full = piece.astype(F32)
            norms.append(jnp.sum(full * full, axis=0, keepdims=True))
        these = pl.ds(h * (docs // 2), docs // 2)
        value = jnp.dot(embf[partner(k), these, :], piece, preferred_element_type=F32)
        dist_ref[these, :] = dist_ref[these, :] + value if k else value

    def gather(i):
        for b in range(PIECES):
            emb_near(i, b)
        scatter("far", far, i)
        for b in range(PIECES):
            emb_far(i, b)
        scatter("near", near, i)

    for i in range(BLOCKS):
        for c in range(PIECES):
            sum_near(i, c)
        mark(2 * i)
        for c in range(PIECES):
            sum_far(i, c)
        embed(i)
        mark(2 * i + 1)
        if i == 0:
            c_x[0].wait_recv()
            c_rx = go(remote(half_slot(XN, 0), half_slot(XN, 0), cs.at[5], cr.at[5], YN, m))
            c_y[1].wait_recv()
            c_ry = go(remote(half_slot(YN, 1), half_slot(YN, 1), cs.at[6], cr.at[6], XN, m))
        if i >= 2:
            gather(i - 2)
    c_x[1].wait_recv()
    c_px = go(remote(slot(XN), slot(XN), cs.at[7], cr.at[7], PC, m))
    c_y[0].wait_recv()
    c_py = go(remote(slot(YN), slot(YN), cs.at[8], cr.at[8], PC, m))
    for k in (0, 2, 4):
        product(0, k)
    gather(2)
    c_rx.wait_recv()
    c_pd0 = go(remote(half_slot(DG, 0), half_slot(DG, 0), cs.at[9], cr.at[9], PC, m))
    c_ry.wait_recv()
    c_pd1 = go(remote(half_slot(DG, 1), half_slot(DG, 1), cs.at[10], cr.at[10], PC, m))
    for k in (6, 1, 3):
        product(0, k)
    gather(3)
    for k in (5, 7):
        product(0, k)
    for k in range(8):
        product(1, k)
    doc_norms = jnp.zeros((docs, 1), F32)
    for b in range(8):
        full = embf[b].astype(F32)
        doc_norms = doc_norms + jnp.sum(full * full, axis=1, keepdims=True)
    dist_ref[...] = doc_norms + sum(norms) - 2.0 * dist_ref[...]

    def add(k, columns):
        value = lax.dot_general(columns, onehot[k], (((0,), (0,)), ((), ())), preferred_element_type=F32)
        sums_ref[...] = sums_ref[...] + value if k else value

    add(0, embf[d])
    for k in (1, 2, 4, 6, 3, 5, 7):
        for i in range(BLOCKS):
            for name in ("far", "near"):
                e_copies[(name, i, k)].wait_recv()
        add(k, own[partner(k)])
    for copy in sends:
        copy.wait_send()
    for i in range(BLOCKS):
        for c in range(PIECES):
            sum_copy(near, i, c, ahead).wait_send()
            emb_copy(far, i, c, ahead).wait_send()

    @pl.when(inner == 1)
    def _():
        for i in range(BLOCKS):
            for c in range(PIECES):
                sum_copy(far, i, c, behind).wait_send()
                emb_copy(near, i, c, behind).wait_send()


def fast_body(pooled, w_out, assignments, ema_sums, ema_counts):
    docs, depth = pooled.shape
    dim = w_out.shape[1]
    centers, feats = ema_sums.shape
    asg8 = jnp.broadcast_to(assignments[None, :], (8, docs))
    vmem = pl.BlockSpec(memory_space=pltpu.VMEM)
    dma = pltpu.SemaphoreType.DMA
    distances, batch_sums, counts = pl.pallas_call(
        kernel,
        out_shape=(
            jax.ShapeDtypeStruct((docs, centers), F32),
            jax.ShapeDtypeStruct((feats, centers), F32),
            jax.ShapeDtypeStruct((8, centers), F32),
        ),
        in_specs=[vmem, pl.BlockSpec(memory_space=pl.ANY), vmem, vmem, vmem],
        out_specs=(vmem, vmem, vmem),
        scratch_shapes=[
            pltpu.VMEM((feats, centers), BF),
            pltpu.VMEM((depth, dim), BF),
            pltpu.VMEM((docs, dim), F32),
            pltpu.VMEM((2, docs // 2, dim), BF),
            pltpu.VMEM((2, docs // 2, dim), BF),
            pltpu.VMEM((8, docs, feats), BF),
            pltpu.VMEM((8, docs, feats), BF),
            pltpu.VMEM((8 * feats, centers), BF),
            pltpu.VMEM((8, 8, docs), jnp.int32),
            pltpu.VMEM((8, docs, centers), BF),
            dma((4,)), dma((11,)), dma((11,)), dma((8,)), dma((8,)),
            dma((2, BLOCKS, PIECES)), dma((2, BLOCKS, PIECES)), dma((2, BLOCKS, PIECES)), dma((2, BLOCKS, PIECES)),
            dma((2, BLOCKS, 8)), dma((2, BLOCKS, 8)),
        ],
        compiler_params=pltpu.CompilerParams(
            collective_id=0, has_side_effects=True, vmem_limit_bytes=60 * 1024 * 1024),
        name="embed_and_assign",
    )(pooled, w_out, ema_sums.T, ema_counts[None, :], asg8)
    return finish(distances, batch_sums.T, counts[0], ema_sums, ema_counts)


def solution(mesh):
    fast = mesh.shape["dp"] == 8 and mesh.shape["mp"] == 4
    return jax.shard_map(
        fast_body if fast else plain_body,
        mesh=mesh,
        in_specs=(P("dp", "mp"), P("mp", None), P("dp"), P("mp", "dp"), P("mp")),
        out_specs=(P("dp", "mp"), P("mp", "dp"), P("mp"), P("mp", "dp")),
        check_vma=False,
    )
```

```python
import functools
import math

import jax
import jax.numpy as jnp
from jax import lax
from jax.experimental import pallas as pl
from jax.experimental.pallas import tpu as pltpu
from jax.sharding import PartitionSpec as P

EPSILON = 1e-06
EMA_DECAY = 0.9
BF = jnp.bfloat16
F32 = jnp.float32
BLOCKS = 4
PIECES = 2


def plain_body(pooled, w_out, assignments, ema_sums, ema_counts):
    partial_value = jnp.dot(pooled, w_out, preferred_element_type=F32)
    projected = lax.psum(partial_value, "mp")
    inverse_norm = 1.0 / jnp.sqrt(jnp.sum(projected * projected, axis=1, keepdims=True) + EPSILON)
    embedded = (projected * inverse_norm).astype(BF)
    local_centers = ema_sums.shape[0]
    doc_rows = embedded.shape[0]
    centers = (ema_sums / ema_counts[:, None]).astype(BF)
    column_piece = lax.all_gather(centers, "dp", axis=1, tiled=True)
    products = lax.dot_general(
        embedded, column_piece, (((1,), (1,)), ((), ())), preferred_element_type=F32
    )
    piece_wide = column_piece.astype(F32)
    center_norms = jnp.sum(piece_wide * piece_wide, axis=1)
    embed_wide = embedded.astype(F32)
    doc_norms = jnp.sum(embed_wide * embed_wide, axis=1)
    distances = doc_norms[:, None] + center_norms[None, :] - 2.0 * products
    first_center = lax.axis_index("mp") * local_centers
    center_ids = first_center + jnp.arange(local_centers, dtype=jnp.int32)
    feature_cols = ema_sums.shape[1]
    every_assign = lax.all_gather(assignments, "dp", axis=0, tiled=True)
    own_columns = lax.all_to_all(embedded, "dp", split_axis=1, concat_axis=0, tiled=True)
    shard_count = lax.axis_size("dp")
    group_size = math.gcd(shard_count, max(1, 2048 // doc_rows))
    block_rows = group_size * doc_rows
    turns = shard_count // group_size

    def add_block(block_index, totals):
        sums_now, counts_now = totals
        block_assign = lax.dynamic_slice_in_dim(every_assign, block_index * block_rows, block_rows, 0)
        block_columns = lax.dynamic_slice_in_dim(own_columns, block_index * block_rows, block_rows, 0)
        one_hot = (block_assign[None, :] == center_ids[:, None]).astype(BF)
        sums_now = sums_now + jnp.dot(one_hot, block_columns, preferred_element_type=F32)
        counts_now = counts_now + jnp.sum(one_hot, axis=1, dtype=F32)
        return (sums_now, counts_now)

    start_sums = (jnp.zeros((local_centers, feature_cols), F32), jnp.zeros((local_centers,), F32))
    batch_sums, batch_counts = lax.fori_loop(0, turns, add_block, start_sums)
    return finish(distances, batch_sums, batch_counts, ema_sums, ema_counts)


def finish(distances, batch_sums, batch_counts, ema_sums, ema_counts):
    new_counts = EMA_DECAY * ema_counts + (1.0 - EMA_DECAY) * batch_counts
    new_sums = EMA_DECAY * ema_sums + (1.0 - EMA_DECAY) * batch_sums
    new_centroids = (new_sums / new_counts[:, None]).astype(BF)
    return (distances, new_sums, new_counts, new_centroids)


def kernel(
    pooled_ref, w_hbm, ema_ref, ema_counts_ref, asg_own,
    dist_ref, sums_ref, counts_ref,
    cent_own, w_ref, pf, outgoing, incoming, embf, own, cent, asg, onehot,
    w_sem, cs, cr, as_, ar, zs, zr, gs, gr, es, er,
):
    d = lax.axis_index("dp")
    m = lax.axis_index("mp")
    docs = pooled_ref.shape[0]
    block = docs // (2 * BLOCKS)
    dim = w_ref.shape[1]
    chunk = dim // 4
    wide = dim // PIECES
    heads = 8 // PIECES
    feats, centers = cent_own.shape
    half = feats // 2
    core, xi, yi = d % 2, (d // 2) % 2, d // 4

    def partner(k):
        return ((yi + k // 4) % 2) * 4 + ((xi + (k // 2) % 2) % 2) * 2 + (core + k % 2) % 2

    near = m // 2
    far = 1 - near
    inner = (m + near) % 2
    ahead = m + 1 - 2 * near
    behind = m - inner * (1 - 2 * near) + (1 - inner) * (1 - 2 * near)
    PC, XN, YN, DG = partner(1), partner(2), partner(4), partner(6)

    def remote(src, dst, ssem, rsem, dp, mp):
        return pltpu.make_async_remote_copy(
            src_ref=src, dst_ref=dst, send_sem=ssem, recv_sem=rsem,
            device_id={"dp": dp, "mp": mp}, device_id_type=pl.DeviceIdType.MESH,
        )

    def cols(c):
        return pl.ds(c * chunk, chunk)

    def pieces(c):
        return pl.ds(c * wide, wide)

    def rows(flow, i):
        return pl.ds(pl.multiple_of((i * 2 + flow) * block, block), block)

    w_copies = []
    for c in range(4):
        w_copies.append(pltpu.make_async_copy(w_hbm.at[:, cols(c)], w_ref.at[:, cols(c)], w_sem.at[c]))
        w_copies[c].start()
    cent_own[...] = (ema_ref[...] / ema_counts_ref[0:1, :]).astype(BF)

    barrier = pltpu.get_barrier_semaphore()
    for k in range(1, 8):
        pl.semaphore_signal(barrier, inc=1, device_id={"dp": partner(k), "mp": m}, device_id_type=pl.DeviceIdType.MESH)
    pl.semaphore_signal(barrier, inc=1, device_id={"dp": d, "mp": ahead}, device_id_type=pl.DeviceIdType.MESH)

    @pl.when(inner == 1)
    def _():
        pl.semaphore_signal(barrier, inc=1, device_id={"dp": d, "mp": behind}, device_id_type=pl.DeviceIdType.MESH)

    pl.semaphore_wait(barrier, 8 + inner)

    def slot(b):
        return cent.at[pl.ds(pl.multiple_of(b * feats, feats), feats), :]

    def half_slot(b, h):
        return cent.at[pl.ds(pl.multiple_of(b * feats + h * half, half), half), :]

    def half_own(h):
        return cent_own.at[pl.ds(h * half, half), :]

    sends = []

    def go(copy):
        copy.start()
        sends.append(copy)
        return copy

    c_x, c_y = {}, {}
    for h in (0, 1):
        c_x[h] = go(remote(half_own(h), half_slot(d, h), cs.at[h], cr.at[h], XN, m))
        g = 1 - h
        c_y[g] = go(remote(half_own(g), half_slot(d, g), cs.at[2 + g], cr.at[2 + g], YN, m))
    c_p = go(remote(cent_own, slot(d), cs.at[4], cr.at[4], PC, m))
    asg_copies = {}
    for k in range(1, 8):
        asg_copies[k] = go(remote(asg_own, asg.at[d], as_.at[k], ar.at[k], partner(k), m))

    def sum_copy(flow, i, c, to):
        at = (flow, pl.ds(i * block, block), pieces(c))
        return remote(outgoing.at[at], incoming.at[at], zs.at[flow, i, c], zr.at[flow, i, c], d, to)

    def put(flow, i, c, value):
        outgoing[flow, pl.ds(i * block, block), pieces(c)] = value.astype(BF)

    def arrived(flow, i, c):
        return pf[rows(flow, i), pieces(c)] + incoming[flow, pl.ds(i * block, block), pieces(c)].astype(F32)

    def begin(i, c):
        @pl.when(inner == 0)
        def _():
            put(near, i, c, pf[rows(near, i), pieces(c)])
            sum_copy(near, i, c, ahead).start()

    for c in range(4):
        w_copies[c].wait()
        pf[:, cols(c)] = jnp.dot(pooled_ref[...], w_ref[:, cols(c)], preferred_element_type=F32)
        if (c + 1) % (4 // PIECES) == 0:
            begin(0, c // (4 // PIECES))
    for i in range(1, BLOCKS):
        for c in range(PIECES):
            begin(i, c)

    def sum_near(i, c):
        @pl.when(inner == 1)
        def _():
            sum_copy(near, i, c, ahead).wait_recv()
            put(near, i, c, arrived(near, i, c))
            sum_copy(near, i, c, ahead).start()

    def sum_far(i, c):
        sum_copy(far, i, c, behind).wait_recv()

        @pl.when(inner == 1)
        def _():
            put(far, i, c, arrived(far, i, c))
            sum_copy(far, i, c, behind).start()

        @pl.when(inner == 0)
        def _():
            pf[rows(far, i), pieces(c)] = arrived(far, i, c)

    def emb_copy(flow, i, b, to):
        ref = embf.at[pl.ds(heads * b, heads), rows(flow, i), :]
        return remote(ref, ref, gs.at[flow, i, b], gr.at[flow, i, b], d, to)

    def embed(i):
        @pl.when(inner == 0)
        def _():
            value = pf[rows(far, i), :]
            inverse = 1.0 / jnp.sqrt(jnp.sum(value * value, axis=1, keepdims=True) + EPSILON)
            value = value * inverse
            for b in range(8):
                embf[b, rows(far, i), :] = value[:, b * feats:(b + 1) * feats].astype(BF)
            for b in range(PIECES):
                emb_copy(far, i, b, ahead).start()

    def emb_near(i, b):
        @pl.when(inner == 1)
        def _():
            emb_copy(far, i, b, ahead).wait_recv()
            emb_copy(far, i, b, ahead).start()

    def emb_far_inner(i, b):
        @pl.when(inner == 1)
        def _():
            emb_copy(near, i, b, behind).wait_recv()
            emb_copy(near, i, b, behind).start()

    def emb_far_end(i, b):
        @pl.when(inner == 0)
        def _():
            emb_copy(near, i, b, behind).wait_recv()

    e_copies = {}

    def scatter(name, flow, i):
        for k in (1, 2, 4, 6, 3, 5, 7):
            e_copies[(name, i, k)] = go(remote(
                embf.at[partner(k), rows(flow, i), :], own.at[d, rows(flow, i), :],
                es.at[flow, i, k], er.at[flow, i, k], partner(k), m))

    def mark(k):
        if k:
            asg_copies[k].wait_recv()
            row = asg[partner(k)][0:1, :]
        else:
            row = asg_own[0:1, :]
        column = jnp.broadcast_to(row, (128, docs)).T
        for j in range(centers // 128):
            ids = m * centers + j * 128 + lax.broadcasted_iota(jnp.int32, (docs, 128), 1)
            onehot[k, :, j * 128:(j + 1) * 128] = jnp.where(ids == column, 1.0, 0.0).astype(BF)
        count = jnp.dot(jnp.ones((8, docs), BF), onehot[k], preferred_element_type=F32)
        counts_ref[...] = counts_ref[...] + count if k else count

    norms = []
    waits = {1: lambda: (c_p,), 3: lambda: (c_px,), 5: lambda: (c_py,), 7: lambda: (c_pd0, c_pd1)}

    def product(h, k):
        if h == 0 and k in waits:
            for copy in waits[k]():
                copy.wait_recv()
        piece = slot(partner(k))[...] if k else cent_own[...]
        if h == 0:
            full = piece.astype(F32)
            norms.append(jnp.sum(full * full, axis=0, keepdims=True))
        these = pl.ds(h * (docs // 2), docs // 2)
        value = jnp.dot(embf[partner(k), these, :], piece, preferred_element_type=F32)
        dist_ref[these, :] = dist_ref[these, :] + value if k else value

    pieces_all = BLOCKS * PIECES
    at_end = 11
    for s in range(pieces_all + at_end):
        if s < pieces_all:
            sum_near(s // PIECES, s % PIECES)
        n = s - 2
        if 0 <= n < pieces_all:
            sum_far(n // PIECES, n % PIECES)
            if n % PIECES == PIECES - 1:
                embed(n // PIECES)
        n = s - 7
        if 0 <= n < pieces_all:
            emb_near(n // PIECES, n % PIECES)
            if n % PIECES == PIECES - 1:
                scatter("far", far, n // PIECES)
        n = s - 9
        if 0 <= n < pieces_all:
            emb_far_inner(n // PIECES, n % PIECES)
        n = s - at_end
        if 0 <= n < pieces_all:
            emb_far_end(n // PIECES, n % PIECES)
            if n % PIECES == PIECES - 1:
                scatter("near", near, n // PIECES)
        if s < 8:
            mark(s)
        if s == 4:
            c_x[0].wait_recv()
            c_rx = go(remote(half_slot(XN, 0), half_slot(XN, 0), cs.at[5], cr.at[5], YN, m))
            c_y[1].wait_recv()
            c_ry = go(remote(half_slot(YN, 1), half_slot(YN, 1), cs.at[6], cr.at[6], XN, m))
        if s == 11:
            c_x[1].wait_recv()
            c_px = go(remote(slot(XN), slot(XN), cs.at[7], cr.at[7], PC, m))
            c_y[0].wait_recv()
            c_py = go(remote(slot(YN), slot(YN), cs.at[8], cr.at[8], PC, m))
        if s == 15:
            c_rx.wait_recv()
            c_pd0 = go(remote(half_slot(DG, 0), half_slot(DG, 0), cs.at[9], cr.at[9], PC, m))
            c_ry.wait_recv()
            c_pd1 = go(remote(half_slot(DG, 1), half_slot(DG, 1), cs.at[10], cr.at[10], PC, m))
        if s >= 14:
            product(0, {14: 0, 15: 2, 16: 4, 17: 6, 18: 1}[s])
    product(0, 3)
    for k in (5, 7):
        product(0, k)
    for k in range(8):
        product(1, k)
    doc_norms = jnp.zeros((docs, 1), F32)
    for b in range(8):
        full = embf[b].astype(F32)
        doc_norms = doc_norms + jnp.sum(full * full, axis=1, keepdims=True)
    dist_ref[...] = doc_norms + sum(norms) - 2.0 * dist_ref[...]

    def add(k, columns):
        value = lax.dot_general(columns, onehot[k], (((0,), (0,)), ((), ())), preferred_element_type=F32)
        sums_ref[...] = sums_ref[...] + value if k else value

    add(0, embf[d])
    for k in (1, 2, 4, 6, 3, 5, 7):
        for i in range(BLOCKS):
            for name in ("far", "near"):
                e_copies[(name, i, k)].wait_recv()
        add(k, own[partner(k)])
    for copy in sends:
        copy.wait_send()
    for i in range(BLOCKS):
        for c in range(PIECES):
            sum_copy(near, i, c, ahead).wait_send()
            emb_copy(far, i, c, ahead).wait_send()

    @pl.when(inner == 1)
    def _():
        for i in range(BLOCKS):
            for c in range(PIECES):
                sum_copy(far, i, c, behind).wait_send()
                emb_copy(near, i, c, behind).wait_send()


def fast_body(pooled, w_out, assignments, ema_sums, ema_counts):
    docs, depth = pooled.shape
    dim = w_out.shape[1]
    centers, feats = ema_sums.shape
    asg8 = jnp.broadcast_to(assignments[None, :], (8, docs))
    vmem = pl.BlockSpec(memory_space=pltpu.VMEM)
    dma = pltpu.SemaphoreType.DMA
    distances, batch_sums, counts = pl.pallas_call(
        kernel,
        out_shape=(
            jax.ShapeDtypeStruct((docs, centers), F32),
            jax.ShapeDtypeStruct((feats, centers), F32),
            jax.ShapeDtypeStruct((8, centers), F32),
        ),
        in_specs=[vmem, pl.BlockSpec(memory_space=pl.ANY), vmem, vmem, vmem],
        out_specs=(vmem, vmem, vmem),
        scratch_shapes=[
            pltpu.VMEM((feats, centers), BF),
            pltpu.VMEM((depth, dim), BF),
            pltpu.VMEM((docs, dim), F32),
            pltpu.VMEM((2, docs // 2, dim), BF),
            pltpu.VMEM((2, docs // 2, dim), BF),
            pltpu.VMEM((8, docs, feats), BF),
            pltpu.VMEM((8, docs, feats), BF),
            pltpu.VMEM((8 * feats, centers), BF),
            pltpu.VMEM((8, 8, docs), jnp.int32),
            pltpu.VMEM((8, docs, centers), BF),
            dma((4,)), dma((11,)), dma((11,)), dma((8,)), dma((8,)),
            dma((2, BLOCKS, PIECES)), dma((2, BLOCKS, PIECES)), dma((2, BLOCKS, PIECES)), dma((2, BLOCKS, PIECES)),
            dma((2, BLOCKS, 8)), dma((2, BLOCKS, 8)),
        ],
        compiler_params=pltpu.CompilerParams(
            collective_id=0, has_side_effects=True, vmem_limit_bytes=60 * 1024 * 1024),
        name="embed_and_assign",
    )(pooled, w_out, ema_sums.T, ema_counts[None, :], asg8)
    return finish(distances, batch_sums.T, counts[0], ema_sums, ema_counts)


def solution(mesh):
    fast = mesh.shape["dp"] == 8 and mesh.shape["mp"] == 4
    return jax.shard_map(
        fast_body if fast else plain_body,
        mesh=mesh,
        in_specs=(P("dp", "mp"), P("mp", None), P("dp"), P("mp", "dp"), P("mp")),
        out_specs=(P("dp", "mp"), P("mp", "dp"), P("mp"), P("mp", "dp")),
        check_vma=False,
    )
```
